32 devices in a mesh: section: 2 (over core), dp: 4 (over z), tensor: 4 (over y, x).
Axes of the slice: x: 2, y: 2, z: 4, core: 2. Of those that a mesh axis runs over, the one named last changes fastest.
Arguments:
- block_input: bfloat16 [4, 512, 2048], P(None, 'dp'), may hold values from -6 to 6
- cotangent: bfloat16 [4, 512, 2048], P(None, 'dp'), may hold values from -6 to 6
- segments: int32 [4, 4, 128], P(None, 'dp'), may hold values from 0 to 3, never falling along the last dimension, each value on 1 to 85 neighbouring positions
- live_rows: int32 [4, 4], P(None, 'dp'), may hold values from 42 to 128, as said below
- attn_gain: float32 [2, 2048], P('section'), may hold values from 0.5 to 1.5
- query_weight: bfloat16 [2, 2048, 2048], P('section', 'dp', 'tensor'), may hold values from -0.125 to 0.125
- key_projection: bfloat16 [2, 2048, 1024], P('section', 'dp', 'tensor'), may hold values from -0.125 to 0.125
- value_projection: bfloat16 [2, 2048, 1024], P('section', 'dp', 'tensor'), may hold values from -0.125 to 0.125
- query_gain: float32 [2, 128], P('section'), may hold values from 0.5 to 1.5
- key_gain: float32 [2, 128], P('section'), may hold values from 0.5 to 1.5
- out_weight: bfloat16 [2, 2048, 2048], P('section', 'tensor', 'dp'), may hold values from -0.5 to 0.5
- mlp_gain: float32 [2, 2048], P('section'), may hold values from 0.5 to 1.5
- gate_weight: bfloat16 [2, 2048, 6144], P('section', 'dp', 'tensor'), may hold values from -0.125 to 0.125
- up_weight: bfloat16 [2, 2048, 6144], P('section', 'dp', 'tensor'), may hold values from -0.125 to 0.125
- down_weight: bfloat16 [2, 6144, 2048], P('section', 'tensor', 'dp'), may hold values from -0.078125 to 0.078125
Outputs:
- block_outputs: bfloat16 [2, 4, 512, 2048], P('section', None, 'dp')
- input_grads: bfloat16 [2, 4, 512, 2048], P('section', None, 'dp')
- attn_gain_grad: float32 [2, 2048], P('section')
- query_weight_grad: float32 [2, 2048, 2048], P('section', 'dp', 'tensor')
- key_weight_grad: float32 [2, 2048, 1024], P('section', 'dp', 'tensor')
- value_weight_grad: float32 [2, 2048, 1024], P('section', 'dp', 'tensor')
- query_gain_grad: float32 [2, 128], P('section')
- key_gain_grad: float32 [2, 128], P('section')
- out_weight_grad: float32 [2, 2048, 2048], P('section', 'tensor', 'dp')
- mlp_gain_grad: float32 [2, 2048], P('section')
- gate_weight_grad: float32 [2, 2048, 6144], P('section', 'dp', 'tensor')
- up_weight_grad: float32 [2, 2048, 6144], P('section', 'dp', 'tensor')
- down_weight_grad: float32 [2, 6144, 2048], P('section', 'tensor', 'dp')
The draws below stay inside these ranges and needn't reach their ends.
Inputs may be any that keep to these rules, and one draw needn't show every extreme that they name: `segments`: within each micro-batch of a data group the numbers never fall; each of the 4 sequences holds 1 to 85 rows, and one holds exactly 85. `live_rows`: in every draw some micro-batch of some data group has all 128 rows live.
All inputs are finite; a program needn't handle non-finite values.
Results may differ from the reference program's by a relative error of at most 0.03.
Values may be sent and summed in bfloat16 or wider, within the bound.
No kernel may reach another device: no remote copies, remote signals or barrier semaphores. Data moves between devices by JAX's collectives and lax.ppermute only.
A program may use at most 256 MiB of HBM per device.

```python
import math
import jax
import jax.numpy as jnp
import numpy as np
from jax import lax

MODEL_WIDTH = 2048
HQ = 16
KEY_VALUE_HEADS = 8
HEAD_SIZE = 128
FF = 6144
ROWS = 128
MB = 4
SEGS = 4
SEQ_MAX = 85
GROUPS = 4
TOK = 512
RELAY_SECTIONS = 2


def draw_live_rows(key, part):
    group_count = TOK // ROWS
    count_key = jax.random.fold_in(key, 11)
    place_key = jax.random.fold_in(key, 23)
    counts = jax.random.randint(count_key, (MB * group_count,), ROWS // 3, ROWS + 1)
    full_spot = jax.random.randint(place_key, (), 0, MB * group_count)
    filled = jnp.where(jnp.arange(MB * group_count) == full_spot, ROWS, counts)
    return filled.reshape(MB, group_count).astype(jnp.int32)


def block_levels(own_key, dims, cuts, low, largest):
    factor_of, own = 1.0, jax.random.fold_in(own_key, 6)
    for dim, blocks in cuts:
        steps = jnp.exp(jax.random.uniform(jax.random.fold_in(own, dim), (blocks,), jnp.float32, low / len(cuts), largest / len(cuts)))
        factor_of = factor_of * jnp.repeat(steps, dims[dim] // blocks).reshape([-1 if axis == dim else 1 for axis in range(len(dims))])
    return factor_of


def split_up(number_of, total, most, lean):
    portions = [(1 << 20) // math.isqrt(standing ** lean) + 1 for standing in range(2, number_of + 1)]
    rest, given = total - most - (number_of - 1), [1] * (number_of - 1)
    while rest > 0:
        candidates = [i for i in range(number_of - 1) if given[i] < most]
        mass, remaining = sum([portions[i] for i in candidates]), rest
        for i in candidates:
            extra = min(most - given[i], max(1, remaining * portions[i] // mass), rest)
            given[i] = given[i] + extra
            rest = rest - extra
    return np.array([most] + given)


def ragged(key, count, total, bound, skew):
    if count == 2:
        one = jax.random.randint(key, (), max(1, total - bound), min(bound, total - 1) + 1)
        return jnp.stack([one, total - one])
    sizes = jnp.asarray(split_up(count, total, bound, skew), jnp.int32)
    pairs = (count - 1) // 2
    donor, receiver = sizes[1:1 + 2 * pairs:2], sizes[2:2 + 2 * pairs:2]
    room = jnp.minimum(donor - 1, bound - receiver)
    shifted = jax.random.randint(jax.random.fold_in(key, 1), (pairs,), 0, 1 << 20) % (room + 1)
    sizes = sizes.at[1:1 + 2 * pairs:2].set(donor - shifted).at[2:2 + 2 * pairs:2].set(receiver + shifted)
    return sizes[jax.random.permutation(jax.random.fold_in(key, 2), count)]


def normal_values(own_key, dims, scale, limit, shards=(), held_as=jnp.bfloat16):
    entries = scale * jax.random.normal(own_key, dims, jnp.float32)
    if shards:
        entries = entries * block_levels(own_key, dims, shards, -0.22, 0.18)
    return jnp.clip(entries, -limit, limit).astype(held_as)


def setup_inputs(seed: int = 0) -> dict:
    streams_of = jax.random.split(jax.random.key(seed), 16)
    return {
        "block_input": normal_values(streams_of[0], (MB, TOK, MODEL_WIDTH), 1.0, 6.0, ((1, 4),)),
        "cotangent": normal_values(streams_of[1], (MB, TOK, MODEL_WIDTH), 1.0, 6.0, ((1, 4),)),
        "segments": jax.vmap(lambda own: jnp.searchsorted(jnp.cumsum(ragged(own, SEGS, ROWS, SEQ_MAX, 2)), jnp.arange(ROWS), side="right"))(jax.random.split(streams_of[2], MB * GROUPS)).reshape((MB, GROUPS, ROWS)).astype(jnp.int32),
        "live_rows": draw_live_rows(jax.random.fold_in(streams_of[15], 71), 0),
        "attn_gain": jnp.clip(1.0 + 0.1 * jax.random.normal(streams_of[4], (RELAY_SECTIONS, MODEL_WIDTH), jnp.float32), 0.5, 1.5),
        "query_weight": normal_values(streams_of[5], (RELAY_SECTIONS, MODEL_WIDTH, HQ * HEAD_SIZE), MODEL_WIDTH ** -0.5, 0.125, ((0, 2), (1, 4), (2, 4))),
        "key_projection": normal_values(streams_of[6], (RELAY_SECTIONS, MODEL_WIDTH, KEY_VALUE_HEADS * HEAD_SIZE), MODEL_WIDTH ** -0.5, 0.125, ((0, 2), (1, 4), (2, 4))),
        "value_projection": normal_values(streams_of[7], (RELAY_SECTIONS, MODEL_WIDTH, KEY_VALUE_HEADS * HEAD_SIZE), MODEL_WIDTH ** -0.5, 0.125, ((0, 2), (1, 4), (2, 4))),
        "query_gain": jnp.clip(1.0 + 0.1 * jax.random.normal(streams_of[8], (RELAY_SECTIONS, HEAD_SIZE), jnp.float32), 0.5, 1.5),
        "key_gain": jnp.clip(1.0 + 0.1 * jax.random.normal(streams_of[9], (RELAY_SECTIONS, HEAD_SIZE), jnp.float32), 0.5, 1.5),
        "out_weight": normal_values(streams_of[10], (RELAY_SECTIONS, HQ * HEAD_SIZE, MODEL_WIDTH), (HQ * HEAD_SIZE // 16) ** -0.5, 0.5, ((0, 2), (1, 4), (2, 4))),
        "mlp_gain": jnp.clip(1.0 + 0.1 * jax.random.normal(streams_of[11], (RELAY_SECTIONS, MODEL_WIDTH), jnp.float32), 0.5, 1.5),
        "gate_weight": normal_values(streams_of[12], (RELAY_SECTIONS, MODEL_WIDTH, FF), MODEL_WIDTH ** -0.5, 0.125, ((0, 2), (1, 4), (2, 4))),
        "up_weight": normal_values(streams_of[13], (RELAY_SECTIONS, MODEL_WIDTH, FF), MODEL_WIDTH ** -0.5, 0.125, ((0, 2), (1, 4), (2, 4))),
        "down_weight": normal_values(streams_of[14], (RELAY_SECTIONS, FF, MODEL_WIDTH), FF ** -0.5, 0.078125, ((0, 2), (1, 4), (2, 4))),
    }


eps_norm = 1e-06
rope_base = 1000000.0

def root_scale(inside, gain_vector):
    mean_square = lax.optimization_barrier(jnp.mean(inside * inside, axis=-1, keepdims=True))
    return inside * lax.rsqrt(mean_square + eps_norm) * gain_vector

def gated_units(gate_proj, up_proj):
    return jax.nn.silu(gate_proj) * up_proj

def layout(segment, live_count):
    row_count = segment.shape[0]
    row_index = jnp.arange(row_count, dtype=jnp.int32)
    same_segment = segment[:, None] == segment[None, :]
    start_row = lax.optimization_barrier(jnp.min(jnp.where(same_segment, row_index[None, :], row_count), axis=1))
    positions = (row_index - start_row).astype(jnp.float32)
    live_row = row_index < live_count
    allowed = same_segment & (row_index[None, :] <= row_index[:, None]) & live_row[:, None] & live_row[None, :] | (row_index[:, None] == row_index[None, :])
    half_size = HEAD_SIZE // 2
    frequency = rope_base ** (-(jnp.arange(half_size).astype(jnp.float32) * (2.0 / HEAD_SIZE)))
    angles = positions[:, None] * frequency[None, :]
    cosine_table = jnp.concatenate([jnp.cos(angles), jnp.cos(angles)], axis=-1)
    sine_table = jnp.concatenate([jnp.sin(angles), jnp.sin(angles)], axis=-1)
    return (allowed, cosine_table, sine_table)

def head_prepare(raw_part, gain_part, cosine_table, sine_table):
    row_count = raw_part.shape[0]
    split_heads = raw_part.reshape(row_count, raw_part.shape[1] // HEAD_SIZE, HEAD_SIZE)
    normed = root_scale(split_heads, gain_part)
    half_size = HEAD_SIZE // 2
    turned = jnp.concatenate([-normed[..., half_size:], normed[..., :half_size]], axis=-1)
    return normed * cosine_table[:, None, :] + turned * sine_table[:, None, :]

def attention_scores(queries, key_heads):
    row_count = queries.shape[0]
    kv_count = key_heads.shape[1]
    grouped = queries.reshape(row_count, kv_count, queries.shape[1] // kv_count, HEAD_SIZE)
    scores = jnp.einsum('qkgd,pkd->kgqp', grouped.astype(jnp.float32), key_heads.astype(jnp.float32)) / math.sqrt(HEAD_SIZE)
    return (grouped, scores)

def forward_block(weights, inputs, segment, live_count):
    attn_gain, query_weight, key_projection, value_projection, query_gain, key_gain, out_weight, mlp_gain, gate_weight, up_weight, down_weight = weights
    row_count = inputs.shape[0]
    allowed, cosine_table, sine_table = layout(segment, live_count)
    residual = inputs.astype(jnp.float32)
    normed = root_scale(residual, attn_gain).astype(jnp.bfloat16)
    query_unnormed = jnp.dot(normed, query_weight, preferred_element_type=jnp.float32)
    key_raw = jnp.dot(normed, key_projection, preferred_element_type=jnp.float32)
    values = jnp.dot(normed, value_projection, preferred_element_type=jnp.float32).astype(jnp.bfloat16)
    values = values.reshape(row_count, -1, HEAD_SIZE)
    queries = head_prepare(query_unnormed, query_gain, cosine_table, sine_table).astype(jnp.bfloat16)
    key_heads = head_prepare(key_raw, key_gain, cosine_table, sine_table).astype(jnp.bfloat16)
    grouped, scores = attention_scores(queries, key_heads)
    where_mask = allowed[None, None]
    exponent_total = lax.optimization_barrier(jnp.sum(jnp.where(where_mask, jnp.exp(scores), 0.0), axis=-1))
    log_total = jnp.log(exponent_total)
    probs_half = jnp.where(where_mask, jnp.exp(scores - log_total[..., None]), 0.0).astype(jnp.bfloat16)
    mixed_heads = jnp.einsum('kgqp,pkd->qkgd', probs_half.astype(jnp.float32), values.astype(jnp.float32))
    mixed_heads = mixed_heads.reshape(row_count, -1).astype(jnp.bfloat16)
    middle = residual + jnp.dot(mixed_heads, out_weight, preferred_element_type=jnp.float32)
    mlp_input = root_scale(middle, mlp_gain).astype(jnp.bfloat16)
    gate_proj = jnp.dot(mlp_input, gate_weight, preferred_element_type=jnp.float32)
    up_proj = jnp.dot(mlp_input, up_weight, preferred_element_type=jnp.float32)
    hidden = gated_units(gate_proj, up_proj).astype(jnp.bfloat16)
    result = (middle + jnp.dot(hidden, down_weight, preferred_element_type=jnp.float32)).astype(jnp.bfloat16)
    saved_state = (residual, normed, query_unnormed, key_raw, queries, key_heads, values, log_total, mixed_heads, middle, mlp_input, gate_proj, up_proj, hidden, allowed, cosine_table, sine_table)
    return (result, saved_state)

def backward_block(weights, saved_state, out_grad):
    attn_gain, query_weight, key_projection, value_projection, query_gain, key_gain, out_weight, mlp_gain, gate_weight, up_weight, down_weight = weights
    residual, normed, query_unnormed, key_raw, queries, key_heads, values, log_total, mixed_heads, middle, mlp_input, gate_proj, up_proj, hidden, allowed, cosine_table, sine_table = saved_state
    row_count = out_grad.shape[0]
    grad_down = jnp.dot(hidden.T, out_grad, preferred_element_type=jnp.float32)
    grad_hidden = jnp.dot(out_grad, down_weight.T, preferred_element_type=jnp.float32)
    _, gate_back = jax.vjp(gated_units, gate_proj, up_proj)
    grad_gate, grad_up = gate_back(grad_hidden)
    grad_gate = grad_gate.astype(jnp.bfloat16)
    grad_up = grad_up.astype(jnp.bfloat16)
    grad_gate_w = jnp.dot(mlp_input.T, grad_gate, preferred_element_type=jnp.float32)
    grad_up_w = jnp.dot(mlp_input.T, grad_up, preferred_element_type=jnp.float32)
    mlp_grad = jnp.dot(grad_gate, gate_weight.T, preferred_element_type=jnp.float32) + jnp.dot(grad_up, up_weight.T, preferred_element_type=jnp.float32)
    _, middle_back = jax.vjp(root_scale, middle, mlp_gain)
    middle_norm, gain_mlp = middle_back(mlp_grad)
    middle_grad = out_grad.astype(jnp.float32) + middle_norm
    middle_half = middle_grad.astype(jnp.bfloat16)
    grad_out_w = jnp.dot(mixed_heads.T, middle_half, preferred_element_type=jnp.float32)
    grad_mixed = jnp.dot(middle_half, out_weight.T, preferred_element_type=jnp.float32).astype(jnp.bfloat16)
    grouped, scores = attention_scores(queries, key_heads)
    where_mask = allowed[None, None]
    attn_probs = jnp.where(where_mask, jnp.exp(scores - log_total[..., None]), 0.0)
    probs_half = attn_probs.astype(jnp.bfloat16)
    grad_grouped = grad_mixed.reshape(grouped.shape).astype(jnp.float32)
    grad_values = jnp.einsum('kgqp,qkgd->pkd', probs_half.astype(jnp.float32), grad_grouped)
    grad_probs = jnp.einsum('qkgd,pkd->kgqp', grad_grouped, values.astype(jnp.float32))
    inner_sum = lax.optimization_barrier(jnp.sum(attn_probs * grad_probs, axis=-1, keepdims=True))
    grad_scores = (attn_probs * (grad_probs - inner_sum)).astype(jnp.bfloat16)
    grad_queries = jnp.einsum('kgqp,pkd->qkgd', grad_scores.astype(jnp.float32), key_heads.astype(jnp.float32)).reshape(queries.shape) / math.sqrt(HEAD_SIZE)
    grad_keys = jnp.einsum('kgqp,qkgd->pkd', grad_scores.astype(jnp.float32), grouped.astype(jnp.float32)) / math.sqrt(HEAD_SIZE)

    def query_side(raw_part, gain_part):
        return head_prepare(raw_part, gain_part, cosine_table, sine_table)
    _, query_back = jax.vjp(query_side, query_unnormed, query_gain)
    grad_qraw, gain_query = query_back(grad_queries)
    _, key_back = jax.vjp(query_side, key_raw, key_gain)
    grad_kraw, gain_key = key_back(grad_keys)
    query_half = grad_qraw.astype(jnp.bfloat16)
    key_half = grad_kraw.astype(jnp.bfloat16)
    value_half = grad_values.reshape(row_count, -1).astype(jnp.bfloat16)
    grad_query_w = jnp.dot(normed.T, query_half, preferred_element_type=jnp.float32)
    grad_key_w = jnp.dot(normed.T, key_half, preferred_element_type=jnp.float32)
    grad_value_w = jnp.dot(normed.T, value_half, preferred_element_type=jnp.float32)
    normed_grad = jnp.dot(query_half, query_weight.T, preferred_element_type=jnp.float32)
    normed_grad = normed_grad + jnp.dot(key_half, key_projection.T, preferred_element_type=jnp.float32)
    normed_grad = normed_grad + jnp.dot(value_half, value_projection.T, preferred_element_type=jnp.float32)
    _, residual_back = jax.vjp(root_scale, residual, attn_gain)
    residual_norm, gain_attn = residual_back(normed_grad)
    in_grad = (middle_grad + residual_norm).astype(jnp.bfloat16)
    grad_terms = (gain_attn, grad_query_w, grad_key_w, grad_value_w, gain_query, gain_key, grad_out_w, gain_mlp, grad_gate_w, grad_up_w, grad_down)
    return (in_grad, grad_terms)

def reference(block_input, cotangent, segments, live_rows, attn_gain, query_weight, key_projection, value_projection, query_gain, key_gain, out_weight, mlp_gain, gate_weight, up_weight, down_weight):
    micro_count, token_count, width = block_input.shape
    group_count = segments.shape[1]
    row_count = segments.shape[2]
    block_count = micro_count * group_count
    inputs = block_input.reshape(block_count, row_count, width)
    cotangents = cotangent.reshape(block_count, row_count, width)
    segment_rows = segments.reshape(block_count, row_count)
    live_counts = live_rows.reshape(block_count)
    params = (attn_gain, query_weight, key_projection, value_projection, query_gain, key_gain, out_weight, mlp_gain, gate_weight, up_weight, down_weight)
    section_first = tuple((weight_array[0] for weight_array in params))
    section_second = tuple((weight_array[1] for weight_array in params))

    def first_pass(carry_value, block_item):
        result, _ = forward_block(section_first, block_item[0], block_item[1], block_item[2])
        return (carry_value, result)
    _, first_out = lax.scan(first_pass, jnp.zeros((), jnp.float32), (inputs, segment_rows, live_counts))

    def make_step(weights):

        def block_step(totals, block_item):
            result, saved_state = forward_block(weights, block_item[0], block_item[1], block_item[2])
            in_grad, grad_terms = backward_block(weights, saved_state, block_item[3])
            summed = tuple((left_term + right_term for left_term, right_term in zip(totals, grad_terms)))
            return (summed, (result, in_grad))
        return block_step
    row_index = jnp.arange(row_count, dtype=jnp.int32)
    live_mask = row_index[None, :] < live_counts[:, None]
    masked = jnp.where(live_mask[:, :, None], cotangents, jnp.zeros_like(cotangents))
    zeros_second = tuple((jnp.zeros(weight_array.shape, jnp.float32) for weight_array in section_second))
    zeros_first = tuple((jnp.zeros(weight_array.shape, jnp.float32) for weight_array in section_first))
    totals_second, (second_out, second_grad) = lax.scan(make_step(section_second), zeros_second, (first_out, segment_rows, live_counts, masked))
    totals_first, (unused_out, first_grad) = lax.scan(make_step(section_first), zeros_first, (inputs, segment_rows, live_counts, second_grad))
    block_outputs = jnp.stack([first_out, second_out]).reshape(2, micro_count, token_count, width)
    input_grads = jnp.stack([first_grad, second_grad]).reshape(2, micro_count, token_count, width)
    stacked = [jnp.stack([totals_first[number], totals_second[number]]) for number in range(11)]
    return (block_outputs, input_grads, stacked[0], stacked[1], stacked[2], stacked[3], stacked[4], stacked[5], stacked[6], stacked[7], stacked[8], stacked[9], stacked[10])
```

```python
import functools
import math

import jax
import jax.numpy as jnp
from jax import lax
from jax.experimental import pallas as pl
from jax.experimental.pallas import tpu as pltpu
from jax.sharding import PartitionSpec as P

HEAD_SIZE = 128

eps_norm = 1e-06
rope_base = 1000000.0
BF = jnp.bfloat16
F32 = jnp.float32


def dot(left, right, left_dim, right_dim):
    return lax.dot_general(
        left, right, (((left_dim,), (right_dim,)), ((), ())), preferred_element_type=F32
    )


def after(value, *others):
    return lax.optimization_barrier((value, others))[0]


def swapped(block):
    count = lax.axis_size("section")
    return lax.ppermute(block, "section", [(a, count - 1 - a) for a in range(count)])


def from_ahead(block, axis, step):
    count = lax.axis_size(axis)
    return lax.ppermute(block, axis, [((a + step) % count, a) for a in range(count)])


def to_ahead(block, axis, step):
    count = lax.axis_size(axis)
    return lax.ppermute(block, axis, [(a, (a + step) % count) for a in range(count)])


def fellow(index, step, count):
    if count & (count - 1) == 0:
        return index ^ step
    return (count + step - index) % count


def with_fellow(block, axis, step):
    count = lax.axis_size(axis)
    return lax.ppermute(block, axis, [(d, fellow(d, step, count)) for d in range(count)])


def exchanged(blocks, axis):
    count, here = lax.axis_size(axis), lax.axis_index(axis)

    def block(k):
        return lax.dynamic_index_in_dim(blocks, k % count, 0, keepdims=False)

    pieces = [block(here)] + [to_ahead(block(here + k), axis, k) for k in range(1, count)]
    ordered = []
    for source in range(count):
        chosen = pieces[0]
        for k in range(1, count):
            chosen = jnp.where((here - k) % count == source, pieces[k], chosen)
        ordered.append(chosen)
    return ordered


def rows_gathered(block, axis):
    count, here = lax.axis_size(axis), lax.axis_index(axis)
    pieces = [with_fellow(block, axis, step) for step in range(count)]
    pieces = [block if count & (count - 1) == 0 else pieces[0]] + pieces[1:]
    ordered = []
    for target in range(count):
        chosen = pieces[0]
        for step in range(1, count):
            chosen = jnp.where(fellow(here, step, count) == target, pieces[step], chosen)
        ordered.append(chosen)
    return jnp.concatenate(ordered, axis=0)


def rows_scattered(part, axis):
    count, here = lax.axis_size(axis), lax.axis_index(axis)
    blocks = part.astype(BF).reshape(count, part.shape[0] // count, part.shape[1])
    first = 1 if count & (count - 1) == 0 else 0
    total = 0.0
    if first:
        total = lax.dynamic_index_in_dim(blocks, here, 0, keepdims=False).astype(F32)
    for step in range(first, count):
        block = lax.dynamic_index_in_dim(blocks, fellow(here, step, count), 0, keepdims=False)
        total = total + with_fellow(block, axis, step).astype(F32)
    return total


def summed_over(part, axis):
    count = lax.axis_size(axis)
    if count & (count - 1):
        return jnp.sum(lax.all_gather(part, axis), axis=0)
    step = 1
    while step < count:
        part = part + with_fellow(part, axis, step)
        step *= 2
    return part


def root_scale(inside, gain_vector):
    mean_square = jnp.mean(inside * inside, axis=-1, keepdims=True)
    return inside * lax.rsqrt(mean_square + eps_norm) * gain_vector


def unit_rows(inside):
    mean_square = jnp.mean(inside * inside, axis=-1, keepdims=True)
    return inside * lax.rsqrt(mean_square + eps_norm)


def gated_units(gate_proj, up_proj):
    return jax.nn.silu(gate_proj) * up_proj


def layout(segment, live_count):
    row_count = segment.shape[0]
    row_index = jnp.arange(row_count, dtype=jnp.int32)
    same_segment = segment[:, None] == segment[None, :]
    start_row = jnp.min(jnp.where(same_segment, row_index[None, :], row_count), axis=1)
    positions = (row_index - start_row).astype(F32)
    live_row = row_index < live_count
    allowed = same_segment & (row_index[None, :] <= row_index[:, None]) & live_row[
        :, None
    ] & live_row[None, :] | (row_index[:, None] == row_index[None, :])
    half_size = HEAD_SIZE // 2
    frequency = rope_base ** (-(jnp.arange(half_size).astype(F32) * (2.0 / HEAD_SIZE)))
    angles = positions[:, None] * frequency[None, :]
    cosine_table = jnp.concatenate([jnp.cos(angles), jnp.cos(angles)], axis=-1)
    sine_table = jnp.concatenate([jnp.sin(angles), jnp.sin(angles)], axis=-1)
    return (allowed, cosine_table, sine_table)


def contract(left, right, left_dim, right_dim):
    return lax.dot_general(
        left, right, (((left_dim,), (right_dim,)), ((), ())), preferred_element_type=F32
    )


def turned(rows):
    half_size = HEAD_SIZE // 2
    lane = lax.broadcasted_iota(jnp.int32, rows.shape, 1)
    rolled = pltpu.roll(rows, half_size, 1)
    return jnp.where(lane < half_size, -rolled, rolled)


def unit_head(raw_part):
    mean_square = jnp.mean(raw_part * raw_part, axis=-1, keepdims=True)
    scale = lax.rsqrt(mean_square + eps_norm)
    return raw_part * scale, scale


def weight_copies(pieces, weight, sems, core, count):
    half = pieces[0].shape[1]
    copies = []
    for number, piece in enumerate(pieces):
        which = core if number % 2 == 0 else 1 - core
        columns = pl.ds(pl.multiple_of(which * half, 128), half)
        copies.append(
            pltpu.make_async_copy(
                piece, weight.at[number // 2, :, columns], sems.at[number]
            )
        )
    return copies


def columns_of(step, place, count, size):
    block = lax.rem(place + step, count)
    return pl.ds(pl.multiple_of(block * size, size), size)


def attn_forward_kernel(count, query_heads, key_heads, block_count, place_ref, *refs):
    pieces = refs[: 2 * count]
    (x_ref, gain_ref, qgain_ref, kgain_ref, cos_ref, sin_ref, mask_ref) = refs[
        2 * count : 2 * count + 7
    ]
    (normed_ref, raw_ref, heads_ref, mixed_ref, part_ref) = refs[2 * count + 7 : 2 * count + 12]
    weight, sems = refs[2 * count + 12 :]
    place, core = place_ref[0], place_ref[1]
    copies = weight_copies(pieces, weight, sems, core, count)
    for copy in copies:
        copy.start()
    x = x_ref[...].astype(F32)
    mean_square = jnp.mean(x * x, axis=-1, keepdims=True)
    normed_ref[...] = (x * lax.rsqrt(mean_square + eps_norm) * gain_ref[...]).astype(BF)
    size = weight.shape[1]
    raw_width = raw_ref.shape[1]
    total = None
    for step in range(count):
        copies[2 * step].wait()
        copies[2 * step + 1].wait()
        term = contract(
            normed_ref[:, columns_of(step, place, count, size)], weight[step, :, :raw_width], 1, 0
        )
        total = term if total is None else total + term
    raw_ref[...] = total
    cosine, sine = cos_ref[...], sin_ref[...]
    for head in range(query_heads + key_heads):
        lanes = slice(head * HEAD_SIZE, (head + 1) * HEAD_SIZE)
        gain = qgain_ref[...] if head < query_heads else kgain_ref[...]
        rows = unit_head(raw_ref[:, lanes])[0] * gain
        heads_ref[:, lanes] = (rows * cosine + turned(rows) * sine).astype(BF)
    start = (query_heads + key_heads) * HEAD_SIZE
    heads_ref[:, start:] = raw_ref[:, start:].astype(BF)
    row_count = x.shape[0] // block_count
    group = query_heads // key_heads
    for block in range(block_count):
        rows = slice(block * row_count, (block + 1) * row_count)
        allowed = mask_ref[rows, :] > 0.5
        for head in range(query_heads):
            lanes = slice(head * HEAD_SIZE, (head + 1) * HEAD_SIZE)
            key_at = (query_heads + head // group) * HEAD_SIZE
            value_at = start + (head // group) * HEAD_SIZE
            scores = contract(
                heads_ref[rows, lanes], heads_ref[rows, key_at : key_at + HEAD_SIZE], 1, 1
            ) / math.sqrt(HEAD_SIZE)
            sums = jnp.sum(jnp.where(allowed, jnp.exp(scores), 0.0), axis=-1, keepdims=True)
            probs = jnp.where(allowed, jnp.exp(scores - jnp.log(sums)), 0.0).astype(BF)
            mixed_ref[rows, lanes] = contract(
                probs, heads_ref[rows, value_at : value_at + HEAD_SIZE], 1, 0
            ).astype(BF)
    for step in range(count):
        part_ref[:, columns_of(step, place, count, size)] = contract(
            mixed_ref[...], weight[step, :, raw_width:], 1, 1
        ).astype(BF)


def attn_backward_kernel(count, query_heads, key_heads, block_count, place_ref, *refs):
    pieces = refs[: 2 * count]
    (half_ref, raw_ref, heads_ref, qgain_ref, kgain_ref, cos_ref, sin_ref, mask_ref) = refs[
        2 * count : 2 * count + 8
    ]
    (halves_ref, part_ref, gains_ref) = refs[2 * count + 8 : 2 * count + 11]
    weight, mixed_grad, head_grad, sems = refs[2 * count + 11 :]
    place, core = place_ref[0], place_ref[1]
    copies = weight_copies(pieces, weight, sems, core, count)
    for copy in copies:
        copy.start()
    size = weight.shape[1]
    raw_width = heads_ref.shape[1]
    total = None
    for step in range(count):
        copies[2 * step].wait()
        copies[2 * step + 1].wait()
        term = contract(
            half_ref[:, columns_of(step, place, count, size)], weight[step, :, raw_width:], 1, 0
        )
        total = term if total is None else total + term
    mixed_grad[...] = total.astype(BF)
    root = math.sqrt(HEAD_SIZE)
    start = (query_heads + key_heads) * HEAD_SIZE
    row_count = half_ref.shape[0] // block_count
    group = query_heads // key_heads
    for block in range(block_count):
        rows = slice(block * row_count, (block + 1) * row_count)
        allowed = mask_ref[rows, :] > 0.5
        for key_head in range(key_heads):
            key_at = (query_heads + key_head) * HEAD_SIZE
            value_at = start + key_head * HEAD_SIZE
            keys = heads_ref[rows, key_at : key_at + HEAD_SIZE]
            values = heads_ref[rows, value_at : value_at + HEAD_SIZE]
            key_total, value_total = None, None
            for head in range(key_head * group, (key_head + 1) * group):
                lanes = slice(head * HEAD_SIZE, (head + 1) * HEAD_SIZE)
                queries, grads = heads_ref[rows, lanes], mixed_grad[rows, lanes]
                scores = contract(queries, keys, 1, 1) / root
                sums = jnp.sum(jnp.where(allowed, jnp.exp(scores), 0.0), axis=-1, keepdims=True)
                probs = jnp.where(allowed, jnp.exp(scores - jnp.log(sums)), 0.0)
                value_term = contract(probs.astype(BF), grads, 0, 0)
                probs_grad = contract(grads, values, 1, 1)
                inner = jnp.sum(probs * probs_grad, axis=-1, keepdims=True)
                scores_grad = (probs * (probs_grad - inner)).astype(BF)
                head_grad[rows, lanes] = contract(scores_grad, keys, 1, 0) / root
                key_term = contract(scores_grad, queries, 0, 0)
                key_total = key_term if key_total is None else key_total + key_term
                value_total = value_term if value_total is None else value_total + value_term
            head_grad[rows, key_at : key_at + HEAD_SIZE] = key_total / root
            halves_ref[rows, value_at : value_at + HEAD_SIZE] = value_total.astype(BF)
    cosine, sine = cos_ref[...], sin_ref[...]
    gain_sums = [None, None]
    for head in range(query_heads + key_heads):
        lanes = slice(head * HEAD_SIZE, (head + 1) * HEAD_SIZE)
        kind = 0 if head < query_heads else 1
        gain = qgain_ref[...] if kind == 0 else kgain_ref[...]
        grad = head_grad[:, lanes]
        scaled_grad = grad * cosine - turned(grad * sine)
        unit, scale = unit_head(raw_ref[:, lanes])
        term = jnp.sum(scaled_grad * unit, axis=0, keepdims=True)
        gain_sums[kind] = term if gain_sums[kind] is None else gain_sums[kind] + term
        unit_grad = scaled_grad * gain
        inner = jnp.mean(unit_grad * unit, axis=-1, keepdims=True)
        halves_ref[:, lanes] = (scale * (unit_grad - unit * inner)).astype(BF)
    gains_ref[0:1, :] = gain_sums[0]
    gains_ref[1:2, :] = gain_sums[1]
    for step in range(count):
        part_ref[:, columns_of(step, place, count, size)] = contract(
            halves_ref[...], weight[step, :, :raw_width], 1, 1
        ).astype(BF)


def weight_grad_kernel(count, place_ref, normed_ref, halves_ref, half_ref, mixed_ref, own_ref, other_ref, grads):
    place, core = place_ref[0], place_ref[1]
    size = own_ref.shape[1]
    raw_width = halves_ref.shape[1]
    half = own_ref.shape[2]
    for step in range(count):
        columns = columns_of(step, place, count, size)
        grads[:, :raw_width] = contract(normed_ref[:, columns], halves_ref[...], 0, 0)
        grads[:, raw_width:] = contract(half_ref[:, columns], mixed_ref[...], 0, 0)
        own = pl.ds(pl.multiple_of(core * half, 128), half)
        other = pl.ds(pl.multiple_of((1 - core) * half, 128), half)
        own_ref[step] = grads[:, own].astype(BF)
        other_ref[step] = grads[:, other].astype(BF)


def vmem(shape, dtype):
    return jax.ShapeDtypeStruct(shape, dtype)


def kernel_call(kernel, place, weights, others, results, scratch, flops):
    in_specs = [pl.BlockSpec(memory_space=pltpu.SMEM)]
    in_specs += [pl.BlockSpec(memory_space=pl.ANY)] * len(weights)
    in_specs += [pl.BlockSpec(memory_space=pltpu.VMEM)] * len(others)
    if weights:
        scratch = (
            [pltpu.VMEM((len(weights) // 2, weights[0].shape[0], 2 * weights[0].shape[1]), BF)]
            + scratch
            + [pltpu.SemaphoreType.DMA((len(weights),))]
        )
    moved = sum(a.size * a.dtype.itemsize for a in (*weights, *others))
    return pl.pallas_call(
        kernel,
        out_shape=results,
        in_specs=in_specs,
        out_specs=[pl.BlockSpec(memory_space=pltpu.VMEM)] * len(results),
        scratch_shapes=scratch,
        cost_estimate=pl.CostEstimate(flops=flops, bytes_accessed=moved, transcendentals=0),
    )(place, *weights, *others)


def per_device(
    block_input,
    cotangent,
    segments,
    live_rows,
    attn_gain,
    query_weight,
    key_projection,
    value_projection,
    query_gain,
    key_gain,
    out_weight,
    mlp_gain,
    gate_weight,
    up_weight,
    down_weight,
):
    sections = lax.axis_size("section")
    dp_count = lax.axis_size("dp")
    tensor_count = lax.axis_size("tensor")
    core = lax.axis_index("section")
    column = lax.axis_index("tensor")
    first_core = core == 0
    micro_count, row_count, width = block_input.shape
    own_count = micro_count // sections
    row_total = own_count * row_count
    quarter = row_total // tensor_count

    def own_blocks(array):
        return lax.dynamic_slice_in_dim(array, core * own_count, own_count, 0)

    def own_quarter(array):
        return lax.dynamic_slice_in_dim(array, column * quarter, quarter, 0)

    small = jnp.concatenate([attn_gain[0], mlp_gain[0], query_gain[0], key_gain[0]])
    small_other = swapped(small)
    gains = []
    for section in range(sections):
        chosen = jnp.where(core == section, small, small_other)
        gains.append(
            (
                chosen[:width],
                chosen[width : 2 * width],
                chosen[2 * width : 2 * width + HEAD_SIZE],
                chosen[2 * width + HEAD_SIZE :],
            )
        )

    hidden_local = gate_weight.shape[2]
    block_width = gate_weight.shape[1]
    part_size = hidden_local // (sections * dp_count)
    split = (sections, dp_count, 1, part_size, block_width)
    gate_up_shard = jnp.concatenate(
        [gate_weight[0].T.reshape(split), up_weight[0].T.reshape(split)], axis=2
    )
    down_shard = down_weight[0].reshape(split)
    attn_shard = jnp.concatenate(
        [query_weight[0], key_projection[0], value_projection[0], out_weight[0].T], axis=1
    )
    query_width, key_width = query_weight.shape[2], key_projection.shape[2]
    raw_width = query_width + 2 * key_width
    attn_columns = attn_shard.shape[1]
    attn_shard = jnp.stack(
        [attn_shard[:, : attn_columns // 2], attn_shard[:, attn_columns // 2 :]]
    )
    query_heads, key_heads = query_width // HEAD_SIZE, key_width // HEAD_SIZE
    place = jnp.stack([lax.axis_index("dp"), core]).astype(jnp.int32)

    def both_sections(shard):
        keep = lax.dynamic_index_in_dim(shard, core, 0, keepdims=False)
        got = swapped(lax.dynamic_index_in_dim(shard, 1 - core, 0, keepdims=False))
        return [jnp.where(core == section, keep, got) for section in range(sections)]

    gate_up_halves = both_sections(gate_up_shard)
    down_halves = both_sections(after(down_shard, gate_up_halves[0]))
    attn_halves = both_sections(after(attn_shard, gate_up_halves[0]))

    def re_laid(half, *deps):
        met = exchanged(after(half, *deps), "dp")
        return jnp.concatenate(met, axis=2)

    def spread(piece):
        return lax.all_gather(piece, "tensor", axis=1, tiled=True).reshape(-1, width)

    def attn_weights(section, *deps):
        half = after(attn_halves[section], *deps)
        pieces = []
        for step in range(dp_count):
            piece = from_ahead(half, "dp", step) if step else half
            pieces += [piece, swapped(piece)]
        return pieces

    def to_mlp_rows(block):
        pieces = [block] + [from_ahead(block, "dp", step) for step in range(1, dp_count)]
        return jnp.concatenate(pieces + [swapped(piece) for piece in pieces], axis=0)

    def from_mlp_rows(own_part, other_part):
        met = own_part + swapped(other_part.astype(BF)).astype(F32)
        total = met[:quarter]
        for step in range(1, dp_count):
            block = met[step * quarter : (step + 1) * quarter].astype(BF)
            total = total + to_ahead(block, "dp", step).astype(F32)
        return total

    half_rows = dp_count * quarter
    gate_up_0 = re_laid(gate_up_halves[0])
    down_0 = re_laid(down_halves[0], gate_up_0)
    attn_w = [attn_weights(0, down_0)]
    gate_up_w, down_w = [spread(gate_up_0)], [spread(down_0)]

    block_input, cotangent, segments, live_rows = after(
        (block_input, cotangent, segments, live_rows), gate_up_halves[0]
    )
    segment_rows = own_blocks(segments[:, 0, :])
    live_counts = own_blocks(live_rows[:, 0])
    allowed, cosine_table, sine_table = jax.vmap(layout)(segment_rows, live_counts)
    tables = (
        cosine_table.reshape(row_total, HEAD_SIZE),
        sine_table.reshape(row_total, HEAD_SIZE),
        allowed.astype(F32).reshape(row_total, row_count),
    )
    kernel_sizes = (dp_count, query_heads, key_heads, own_count)
    attn_flops = 2 * row_total * width * attn_columns

    current = own_blocks(block_input).reshape(row_total, width)
    current_quarter = own_quarter(current).astype(F32)
    live = (jnp.arange(row_count)[None, :] < live_counts[:, None]).reshape(row_total, 1)
    last_grad = own_blocks(cotangent).reshape(row_total, width)
    last_grad = own_quarter(jnp.where(live, last_grad, jnp.zeros_like(last_grad)))

    outputs, kept_attn, kept_mlp = [], [], []
    for section in range(sections):
        gain_attn, gain_mlp, gain_query, gain_key = gains[section]
        weight = attn_w[section]
        following = section + 1 < sections
        if following:
            next_gate_up = re_laid(gate_up_halves[section + 1], *weight)
        else:
            grad_rows = to_mlp_rows(after(last_grad, *weight))
        normed, raw, heads, mixed, attn_part = kernel_call(
            functools.partial(attn_forward_kernel, *kernel_sizes),
            place,
            weight,
            (current, gain_attn[None], gain_query[None], gain_key[None], *tables),
            [
                vmem((row_total, width), BF),
                vmem((row_total, raw_width), F32),
                vmem((row_total, raw_width), BF),
                vmem((row_total, query_width), BF),
                vmem((row_total, width), BF),
            ],
            [],
            attn_flops,
        )
        middle = current_quarter + rows_scattered(attn_part, "tensor")
        mlp_input = root_scale(middle, gain_mlp).astype(BF)
        if following:
            mlp_input, next_gate_up = lax.optimization_barrier((mlp_input, next_gate_up))
        rows = to_mlp_rows(mlp_input)
        if following:
            gate_up_w.append(spread(next_gate_up))
            next_down = re_laid(down_halves[section + 1], mlp_input, next_gate_up)
        projected = dot(rows, gate_up_w[section], 1, 1)
        hidden_count = projected.shape[1] // 2
        gate_proj, up_proj = projected[:, :hidden_count], projected[:, hidden_count:]
        hidden = gated_units(gate_proj, up_proj).astype(BF)
        other_part = dot(hidden[half_rows:], down_w[section], 1, 0)
        own_part = dot(hidden[:half_rows], down_w[section], 1, 0)
        if following:
            own_part, next_down = lax.optimization_barrier((own_part, next_down))
            down_w.append(spread(next_down))
            attn_w.append(attn_weights(section + 1, own_part))
        kept_attn.append((normed, raw, heads, mixed, current_quarter))
        kept_mlp.append((middle, rows, gate_proj, up_proj, hidden))
        result = (middle + from_mlp_rows(own_part, other_part)).astype(BF)
        current = rows_gathered(result, "tensor")
        current_quarter = result.astype(F32)
        outputs.append(current)

    def reduced(matrix_grad):
        shaped = matrix_grad.reshape(-1, tensor_count * part_size, width)
        met = lax.psum_scatter(shaped, "tensor", scatter_dimension=1, tiled=True)
        return jnp.stack(
            [met[:, :, k * block_width : (k + 1) * block_width] for k in range(dp_count)]
        )

    out_grad = last_grad
    grads_out, gain_sums, attn_totals, mlp_totals = [], [], [], []
    waiting = None
    for section in reversed(range(sections)):
        gain_attn, gain_mlp, gain_query, gain_key = gains[section]
        gate_up, down = gate_up_w[section], down_w[section]
        weight = attn_w[section]
        middle, rows, gate_proj, up_proj, hidden = kept_mlp[section]
        normed, raw, heads, mixed, inside = kept_attn[section]
        grad_hidden = dot(grad_rows, down, 1, 1)
        _, gate_back = jax.vjp(gated_units, gate_proj, up_proj)
        grad_gate, grad_up = gate_back(grad_hidden)
        grad_gate_up = jnp.concatenate([grad_gate.astype(BF), grad_up.astype(BF)], axis=1)
        other_part = dot(grad_gate_up[half_rows:], gate_up, 1, 0)
        own_part = dot(grad_gate_up[:half_rows], gate_up, 1, 0)
        mlp_grad = from_mlp_rows(own_part, other_part)
        down_dot = dot(hidden, grad_rows, 0, 0).astype(BF)
        gate_up_dot = dot(grad_gate_up, rows, 0, 0).astype(BF)
        down_reduced = reduced(down_dot)
        gate_up_reduced = reduced(gate_up_dot)
        down_total = exchanged(down_reduced, "dp")
        mlp_grad = after(mlp_grad, down_dot, gate_up_dot)

        gain_mlp_sum = jnp.sum(mlp_grad * unit_rows(middle), axis=0)
        _, middle_back = jax.vjp(lambda u: root_scale(u, gain_mlp), middle)
        middle_grad = out_grad.astype(F32) + middle_back(mlp_grad)[0]
        middle_half = middle_grad.astype(BF)
        if waiting is not None:
            middle_half, waiting = lax.optimization_barrier((middle_half, waiting))
        middle_half = rows_gathered(middle_half, "tensor")
        halves, normed_part, head_gains = kernel_call(
            functools.partial(attn_backward_kernel, *kernel_sizes),
            place,
            weight,
            (middle_half, raw, heads, gain_query[None], gain_key[None], *tables),
            [
                vmem((row_total, raw_width), BF),
                vmem((row_total, width), BF),
                vmem((2, HEAD_SIZE), F32),
            ],
            [
                pltpu.VMEM((row_total, query_width), BF),
                pltpu.VMEM((row_total, query_width + key_width), F32),
            ],
            2 * attn_flops,
        )
        gain_query_sum, gain_key_sum = head_gains[0], head_gains[1]
        normed_grad = rows_scattered(normed_part, "tensor")
        own_grad, other_grad = kernel_call(
            functools.partial(weight_grad_kernel, dp_count),
            place,
            (),
            (normed, halves, middle_half, mixed),
            [vmem((dp_count, block_width, attn_columns // 2), BF)] * 2,
            [pltpu.VMEM((block_width, attn_columns), F32)],
            attn_flops,
        )
        attn_chip = own_grad.astype(F32) + swapped(other_grad).astype(F32)
        attn_chip = attn_chip.astype(BF)
        normed_grad = after(normed_grad, attn_chip)
        gain_attn_sum = jnp.sum(normed_grad * unit_rows(inside), axis=0)
        _, inside_back = jax.vjp(lambda u: root_scale(u, gain_attn), inside)
        out_grad = (middle_grad + inside_back(normed_grad)[0]).astype(BF)
        grads_out.append(rows_gathered(out_grad, "tensor"))
        gain_sums.append(
            jnp.concatenate([gain_attn_sum, gain_mlp_sum, gain_query_sum, gain_key_sum])
        )
        if section:
            grad_rows = to_mlp_rows(out_grad)
            gate_up_total = exchanged(after(gate_up_reduced, out_grad), "dp")
        else:
            gate_up_total = exchanged(gate_up_reduced, "dp")
        attn_total = attn_chip[0].astype(F32)
        for step in range(1, dp_count):
            attn_total = attn_total + to_ahead(attn_chip[step], "dp", step).astype(F32)
        attn_totals.append(attn_total)
        gate_up_total, down_total = jnp.stack(gate_up_total), jnp.stack(down_total)
        mlp_totals.append([gate_up_total, down_total])
        if section:
            waiting = (gate_up_total, down_total)
        else:
            mlp_totals[0] = list(waiting)
    for held in (grads_out, gain_sums, attn_totals, mlp_totals):
        held.reverse()

    def to_owner(pair):
        keep = jnp.where(first_core, pair[0], pair[1])
        got = swapped(jnp.where(first_core, pair[1], pair[0]))
        return jnp.where(first_core, keep, got), jnp.where(first_core, got, keep)

    def gathered_output(parts):
        both = jnp.concatenate(to_owner(parts), axis=0)
        return both.reshape(1, micro_count, row_count, width)

    section_outputs = gathered_output(outputs)
    section_grads = gathered_output(grads_out)
    gain_total = jnp.stack(gain_sums)
    for axis in ("section", "tensor", "dp"):
        gain_total = summed_over(gain_total, axis)
    gain_total = jnp.where(first_core, gain_total[0], gain_total[1])[None]

    attn_both = jnp.concatenate(to_owner([t.astype(BF) for t in attn_totals]), axis=1)
    attn_both = attn_both.astype(F32)
    query_grad = attn_both[:, :query_width]
    key_grad = attn_both[:, query_width : query_width + key_width]
    value_grad = attn_both[:, query_width + key_width : raw_width]
    out_grad_w = attn_both[:, raw_width:].T

    def mlp_output(which):
        both = jnp.stack(to_owner([totals[which] for totals in mlp_totals]))
        both = jnp.moveaxis(both, 2, 0)
        return both.reshape(both.shape[0], hidden_local, block_width)

    gate_up_grad = mlp_output(0)
    down_grad = mlp_output(1)
    return (
        section_outputs,
        section_grads,
        gain_total[:, :width],
        query_grad[None],
        key_grad[None],
        value_grad[None],
        gain_total[:, 2 * width : 2 * width + HEAD_SIZE],
        gain_total[:, 2 * width + HEAD_SIZE :],
        out_grad_w[None],
        gain_total[:, width : 2 * width],
        gate_up_grad[0].T.astype(F32)[None],
        gate_up_grad[1].T.astype(F32)[None],
        down_grad[0].astype(F32)[None],
    )


def solution(mesh):
    in_specs = (
        P(None, "dp", None),
        P(None, "dp", None),
        P(None, "dp", None),
        P(None, "dp"),
        P("section", None),
        P("section", "dp", "tensor"),
        P("section", "dp", "tensor"),
        P("section", "dp", "tensor"),
        P("section", None),
        P("section", None),
        P("section", "tensor", "dp"),
        P("section", None),
        P("section", "dp", "tensor"),
        P("section", "dp", "tensor"),
        P("section", "tensor", "dp"),
    )
    out_specs = (
        P("section", None, "dp", None),
        P("section", None, "dp", None),
        P("section", None),
        P("section", "dp", "tensor"),
        P("section", "dp", "tensor"),
        P("section", "dp", "tensor"),
        P("section", None),
        P("section", None),
        P("section", "tensor", "dp"),
        P("section", None),
        P("section", "dp", "tensor"),
        P("section", "dp", "tensor"),
        P("section", "tensor", "dp"),
    )
    return jax.shard_map(
        per_device, mesh=mesh, in_specs=in_specs, out_specs=out_specs, check_vma=False
    )
```

```python
import functools
import math

import jax
import jax.numpy as jnp
from jax import lax
from jax.experimental import pallas as pl
from jax.experimental.pallas import tpu as pltpu
from jax.sharding import PartitionSpec as P


HEAD_SIZE = 128

eps_norm = 1e-06
rope_base = 1000000.0
BF = jnp.bfloat16
F32 = jnp.float32


def dot(left, right, left_dim, right_dim):
    return lax.dot_general(
        left, right, (((left_dim,), (right_dim,)), ((), ())), preferred_element_type=F32
    )


def after(value, *others):
    return lax.optimization_barrier((value, others))[0]


def swapped(block):
    count = lax.axis_size("section")
    return lax.ppermute(block, "section", [(a, count - 1 - a) for a in range(count)])


def from_ahead(block, axis, step):
    count = lax.axis_size(axis)
    return lax.ppermute(block, axis, [((a + step) % count, a) for a in range(count)])


def to_ahead(block, axis, step):
    count = lax.axis_size(axis)
    return lax.ppermute(block, axis, [(a, (a + step) % count) for a in range(count)])


def fellow(index, step, count):
    if count & (count - 1) == 0:
        return index ^ step
    return (count + step - index) % count


def with_fellow(block, axis, step):
    count = lax.axis_size(axis)
    return lax.ppermute(block, axis, [(d, fellow(d, step, count)) for d in range(count)])


def sent_over(blocks, axis):
    count, here = lax.axis_size(axis), lax.axis_index(axis)

    def block(k):
        return lax.dynamic_index_in_dim(blocks, k % count, 0, keepdims=False)

    sent = [to_ahead(block(here + k), axis, k) for k in range(1, count)]
    return [block(here)] + sent


def in_order(pieces, axis):
    count, here = lax.axis_size(axis), lax.axis_index(axis)
    ordered = []
    for source in range(count):
        chosen = pieces[0]
        for k in range(1, count):
            chosen = jnp.where((here - k) % count == source, pieces[k], chosen)
        ordered.append(chosen)
    return ordered


def exchanged(blocks, axis):
    return in_order(sent_over(blocks, axis), axis)


def rows_gathered(block, axis):
    count, here = lax.axis_size(axis), lax.axis_index(axis)
    pieces = [with_fellow(block, axis, step) for step in range(count)]
    pieces = [block if count & (count - 1) == 0 else pieces[0]] + pieces[1:]
    ordered = []
    for target in range(count):
        chosen = pieces[0]
        for step in range(1, count):
            chosen = jnp.where(fellow(here, step, count) == target, pieces[step], chosen)
        ordered.append(chosen)
    return jnp.concatenate(ordered, axis=0)


def rows_scattered(part, axis):
    count, here = lax.axis_size(axis), lax.axis_index(axis)
    blocks = part.astype(BF).reshape(count, part.shape[0] // count, part.shape[1])
    first = 1 if count & (count - 1) == 0 else 0
    total = 0.0
    if first:
        total = lax.dynamic_index_in_dim(blocks, here, 0, keepdims=False).astype(F32)
    for step in range(first, count):
        block = lax.dynamic_index_in_dim(blocks, fellow(here, step, count), 0, keepdims=False)
        met = with_fellow(block, axis, step)
        total = total + met.astype(F32)
    return total


def summed_over(part, axis):
    count = lax.axis_size(axis)
    if count & (count - 1):
        return jnp.sum(lax.all_gather(part, axis), axis=0)
    step = 1
    while step < count:
        met = with_fellow(part, axis, step)
        part = part + met
        step *= 2
    return part


def root_scale(inside, gain_vector):
    mean_square = jnp.mean(inside * inside, axis=-1, keepdims=True)
    return inside * lax.rsqrt(mean_square + eps_norm) * gain_vector


def unit_rows(inside):
    mean_square = jnp.mean(inside * inside, axis=-1, keepdims=True)
    return inside * lax.rsqrt(mean_square + eps_norm)


def gated_units(gate_proj, up_proj):
    return jax.nn.silu(gate_proj) * up_proj


def layout(segment, live_count):
    row_count = segment.shape[0]
    row_index = jnp.arange(row_count, dtype=jnp.int32)
    same_segment = segment[:, None] == segment[None, :]
    start_row = jnp.min(jnp.where(same_segment, row_index[None, :], row_count), axis=1)
    positions = (row_index - start_row).astype(F32)
    live_row = row_index < live_count
    allowed = same_segment & (row_index[None, :] <= row_index[:, None]) & live_row[
        :, None
    ] & live_row[None, :] | (row_index[:, None] == row_index[None, :])
    half_size = HEAD_SIZE // 2
    frequency = rope_base ** (-(jnp.arange(half_size).astype(F32) * (2.0 / HEAD_SIZE)))
    angles = positions[:, None] * frequency[None, :]
    cosine_table = jnp.concatenate([jnp.cos(angles), jnp.cos(angles)], axis=-1)
    sine_table = jnp.concatenate([jnp.sin(angles), jnp.sin(angles)], axis=-1)
    return (allowed, cosine_table, sine_table)


def contract(left, right, left_dim, right_dim):
    return lax.dot_general(
        left, right, (((left_dim,), (right_dim,)), ((), ())), preferred_element_type=F32
    )


def turned(rows):
    half_size = HEAD_SIZE // 2
    lane = lax.broadcasted_iota(jnp.int32, rows.shape, 1)
    rolled = pltpu.roll(rows, half_size, 1)
    return jnp.where(lane < half_size, -rolled, rolled)


def unit_head(raw_part):
    mean_square = jnp.mean(raw_part * raw_part, axis=-1, keepdims=True)
    scale = lax.rsqrt(mean_square + eps_norm)
    return raw_part * scale, scale


def weight_copies(pieces, weight, sems, core):
    half = pieces[0].shape[1]
    copies = []
    for number, piece in enumerate(pieces):
        which = core if number % 2 == 0 else 1 - core
        columns = pl.ds(pl.multiple_of(which * half, 128), half)
        copies.append(
            pltpu.make_async_copy(
                piece, weight.at[number // 2, :, columns], sems.at[number]
            )
        )
    return copies


def columns_of(step, place, count, size):
    block = lax.rem(place + step, count)
    return pl.ds(pl.multiple_of(block * size, size), size)


def attn_forward_kernel(count, query_heads, key_heads, block_count, place_ref, *refs):
    pieces = refs[: 2 * count]
    (x_ref, gain_ref, qgain_ref, kgain_ref, cos_ref, sin_ref, mask_ref) = refs[
        2 * count : 2 * count + 7
    ]
    (normed_ref, raw_ref, heads_ref, mixed_ref, part_ref) = refs[2 * count + 7 : 2 * count + 12]
    weight, sems = refs[2 * count + 12 :]
    place, core = place_ref[0], place_ref[1]
    copies = weight_copies(pieces, weight, sems, core)
    for copy in copies:
        copy.start()
    x = x_ref[...].astype(F32)
    mean_square = jnp.mean(x * x, axis=-1, keepdims=True)
    normed_ref[...] = (x * lax.rsqrt(mean_square + eps_norm) * gain_ref[...]).astype(BF)
    size = weight.shape[1]
    raw_width = raw_ref.shape[1]
    total = None
    for step in range(count):
        copies[2 * step].wait()
        copies[2 * step + 1].wait()
        term = contract(
            normed_ref[:, columns_of(step, place, count, size)], weight[step, :, :raw_width], 1, 0
        )
        total = term if total is None else total + term
    raw_ref[...] = total
    cosine, sine = cos_ref[...], sin_ref[...]
    for head in range(query_heads + key_heads):
        lanes = slice(head * HEAD_SIZE, (head + 1) * HEAD_SIZE)
        gain = qgain_ref[...] if head < query_heads else kgain_ref[...]
        rows = unit_head(raw_ref[:, lanes])[0] * gain
        heads_ref[:, lanes] = (rows * cosine + turned(rows) * sine).astype(BF)
    start = (query_heads + key_heads) * HEAD_SIZE
    heads_ref[:, start:] = raw_ref[:, start:].astype(BF)
    row_count = x.shape[0] // block_count
    group = query_heads // key_heads
    for block in range(block_count):
        rows = slice(block * row_count, (block + 1) * row_count)
        allowed = mask_ref[rows, :] > 0.5
        for head in range(query_heads):
            lanes = slice(head * HEAD_SIZE, (head + 1) * HEAD_SIZE)
            key_at = (query_heads + head // group) * HEAD_SIZE
            value_at = start + (head // group) * HEAD_SIZE
            scores = contract(
                heads_ref[rows, lanes], heads_ref[rows, key_at : key_at + HEAD_SIZE], 1, 1
            ) / math.sqrt(HEAD_SIZE)
            sums = jnp.sum(jnp.where(allowed, jnp.exp(scores), 0.0), axis=-1, keepdims=True)
            probs = jnp.where(allowed, jnp.exp(scores - jnp.log(sums)), 0.0).astype(BF)
            mixed_ref[rows, lanes] = contract(
                probs, heads_ref[rows, value_at : value_at + HEAD_SIZE], 1, 0
            ).astype(BF)
    for step in range(count):
        part_ref[:, columns_of(step, place, count, size)] = contract(
            mixed_ref[...], weight[step, :, raw_width:], 1, 1
        ).astype(BF)


def attn_backward_kernel(count, query_heads, key_heads, block_count, place_ref, *refs):
    pieces = refs[: 2 * count]
    (half_ref, raw_ref, heads_ref, qgain_ref, kgain_ref, cos_ref, sin_ref, mask_ref) = refs[
        2 * count : 2 * count + 8
    ]
    (halves_ref, part_ref, gains_ref) = refs[2 * count + 8 : 2 * count + 11]
    weight, mixed_grad, head_grad, sems = refs[2 * count + 11 :]
    place, core = place_ref[0], place_ref[1]
    copies = weight_copies(pieces, weight, sems, core)
    for copy in copies:
        copy.start()
    size = weight.shape[1]
    raw_width = heads_ref.shape[1]
    total = None
    for step in range(count):
        copies[2 * step].wait()
        copies[2 * step + 1].wait()
        term = contract(
            half_ref[:, columns_of(step, place, count, size)], weight[step, :, raw_width:], 1, 0
        )
        total = term if total is None else total + term
    mixed_grad[...] = total.astype(BF)
    root = math.sqrt(HEAD_SIZE)
    start = (query_heads + key_heads) * HEAD_SIZE
    row_count = half_ref.shape[0] // block_count
    group = query_heads // key_heads
    for block in range(block_count):
        rows = slice(block * row_count, (block + 1) * row_count)
        allowed = mask_ref[rows, :] > 0.5
        for key_head in range(key_heads):
            key_at = (query_heads + key_head) * HEAD_SIZE
            value_at = start + key_head * HEAD_SIZE
            keys = heads_ref[rows, key_at : key_at + HEAD_SIZE]
            values = heads_ref[rows, value_at : value_at + HEAD_SIZE]
            key_total, value_total = None, None
            for head in range(key_head * group, (key_head + 1) * group):
                lanes = slice(head * HEAD_SIZE, (head + 1) * HEAD_SIZE)
                queries, grads = heads_ref[rows, lanes], mixed_grad[rows, lanes]
                scores = contract(queries, keys, 1, 1) / root
                sums = jnp.sum(jnp.where(allowed, jnp.exp(scores), 0.0), axis=-1, keepdims=True)
                probs = jnp.where(allowed, jnp.exp(scores - jnp.log(sums)), 0.0)
                value_term = contract(probs.astype(BF), grads, 0, 0)
                probs_grad = contract(grads, values, 1, 1)
                inner = jnp.sum(probs * probs_grad, axis=-1, keepdims=True)
                scores_grad = (probs * (probs_grad - inner)).astype(BF)
                head_grad[rows, lanes] = contract(scores_grad, keys, 1, 0) / root
                key_term = contract(scores_grad, queries, 0, 0)
                key_total = key_term if key_total is None else key_total + key_term
                value_total = value_term if value_total is None else value_total + value_term
            head_grad[rows, key_at : key_at + HEAD_SIZE] = key_total / root
            halves_ref[rows, value_at : value_at + HEAD_SIZE] = value_total.astype(BF)
    cosine, sine = cos_ref[...], sin_ref[...]
    gain_sums = [None, None]
    for head in range(query_heads + key_heads):
        lanes = slice(head * HEAD_SIZE, (head + 1) * HEAD_SIZE)
        kind = 0 if head < query_heads else 1
        gain = qgain_ref[...] if kind == 0 else kgain_ref[...]
        grad = head_grad[:, lanes]
        scaled_grad = grad * cosine - turned(grad * sine)
        unit, scale = unit_head(raw_ref[:, lanes])
        term = jnp.sum(scaled_grad * unit, axis=0, keepdims=True)
        gain_sums[kind] = term if gain_sums[kind] is None else gain_sums[kind] + term
        unit_grad = scaled_grad * gain
        inner = jnp.mean(unit_grad * unit, axis=-1, keepdims=True)
        halves_ref[:, lanes] = (scale * (unit_grad - unit * inner)).astype(BF)
    gains_ref[0:1, :] = gain_sums[0]
    gains_ref[1:2, :] = gain_sums[1]
    for step in range(count):
        part_ref[:, columns_of(step, place, count, size)] = contract(
            halves_ref[...], weight[step, :, :raw_width], 1, 1
        ).astype(BF)


def weight_grad_kernel(count, place_ref, normed_ref, halves_ref, half_ref, mixed_ref, own_ref, other_ref, grads):
    place, core = place_ref[0], place_ref[1]
    size = own_ref.shape[1]
    raw_width = halves_ref.shape[1]
    half = own_ref.shape[2]
    for step in range(count):
        columns = columns_of(step, place, count, size)
        grads[:, :raw_width] = contract(normed_ref[:, columns], halves_ref[...], 0, 0)
        grads[:, raw_width:] = contract(half_ref[:, columns], mixed_ref[...], 0, 0)
        own = pl.ds(pl.multiple_of(core * half, 128), half)
        other = pl.ds(pl.multiple_of((1 - core) * half, 128), half)
        own_ref[step] = grads[:, own].astype(BF)
        other_ref[step] = grads[:, other].astype(BF)


def vmem(shape, dtype):
    return jax.ShapeDtypeStruct(shape, dtype)


def kernel_call(kernel, place, weights, others, results, scratch, flops):
    in_specs = [pl.BlockSpec(memory_space=pltpu.SMEM)]
    in_specs += [pl.BlockSpec(memory_space=pl.ANY)] * len(weights)
    in_specs += [pl.BlockSpec(memory_space=pltpu.VMEM)] * len(others)
    if weights:
        scratch = (
            [pltpu.VMEM((len(weights) // 2, weights[0].shape[0], 2 * weights[0].shape[1]), BF)]
            + scratch
            + [pltpu.SemaphoreType.DMA((len(weights),))]
        )
    moved = sum(a.size * a.dtype.itemsize for a in (*weights, *others))
    return pl.pallas_call(
        kernel,
        out_shape=results,
        in_specs=in_specs,
        out_specs=[pl.BlockSpec(memory_space=pltpu.VMEM)] * len(results),
        scratch_shapes=scratch,
        cost_estimate=pl.CostEstimate(flops=flops, bytes_accessed=moved, transcendentals=0),
    )(place, *weights, *others)


def per_device(
    block_input,
    cotangent,
    segments,
    live_rows,
    attn_gain,
    query_weight,
    key_projection,
    value_projection,
    query_gain,
    key_gain,
    out_weight,
    mlp_gain,
    gate_weight,
    up_weight,
    down_weight,
):
    sections = lax.axis_size("section")
    dp_count = lax.axis_size("dp")
    tensor_count = lax.axis_size("tensor")
    core = lax.axis_index("section")
    column = lax.axis_index("tensor")
    first_core = core == 0
    micro_count, row_count, width = block_input.shape
    own_count = micro_count // sections
    row_total = own_count * row_count
    quarter = row_total // tensor_count

    def own_blocks(array):
        return lax.dynamic_slice_in_dim(array, core * own_count, own_count, 0)

    def own_quarter(array):
        return lax.dynamic_slice_in_dim(array, column * quarter, quarter, 0)

    small = jnp.concatenate([attn_gain[0], mlp_gain[0], query_gain[0], key_gain[0]])
    small_other = swapped(small)
    gains = []
    for section in range(sections):
        chosen = jnp.where(core == section, small, small_other)
        gains.append(
            (
                chosen[:width],
                chosen[width : 2 * width],
                chosen[2 * width : 2 * width + HEAD_SIZE],
                chosen[2 * width + HEAD_SIZE :],
            )
        )

    hidden_local = gate_weight.shape[2]
    block_width = gate_weight.shape[1]
    part_size = hidden_local // (sections * dp_count)
    split = (sections, dp_count, 1, part_size, block_width)
    gate_up_shard = jnp.concatenate(
        [gate_weight[0].T.reshape(split), up_weight[0].T.reshape(split)], axis=2
    )
    down_shard = down_weight[0].reshape(split)
    attn_shard = jnp.concatenate(
        [query_weight[0], key_projection[0], value_projection[0], out_weight[0].T], axis=1
    )
    query_width, key_width = query_weight.shape[2], key_projection.shape[2]
    raw_width = query_width + 2 * key_width
    attn_columns = attn_shard.shape[1]
    attn_shard = jnp.stack(
        [attn_shard[:, : attn_columns // 2], attn_shard[:, attn_columns // 2 :]]
    )
    query_heads, key_heads = query_width // HEAD_SIZE, key_width // HEAD_SIZE
    place = jnp.stack([lax.axis_index("dp"), core]).astype(jnp.int32)

    def both_sections(shard):
        keep = lax.dynamic_index_in_dim(shard, core, 0, keepdims=False)
        got = swapped(lax.dynamic_index_in_dim(shard, 1 - core, 0, keepdims=False))
        return [jnp.where(core == section, keep, got) for section in range(sections)]

    gate_up_halves = both_sections(gate_up_shard)
    down_halves = both_sections(after(down_shard, gate_up_halves[0]))
    attn_halves = both_sections(after(attn_shard, gate_up_halves[0]))

    def re_laid(half, *deps):
        return sent_over(after(half, *deps), "dp")

    def arrived(pieces, *deps):
        return jnp.concatenate(in_order(after(pieces, *deps), "dp"), axis=2)

    def spread(piece):
        return lax.all_gather(piece, "tensor", axis=1, tiled=True).reshape(-1, width)

    def attn_weights(section, *deps):
        half = after(attn_halves[section], *deps)
        pieces = []
        for step in range(dp_count):
            piece = from_ahead(half, "dp", step) if step else half
            pieces += [piece, swapped(piece)]
        return pieces

    def to_mlp_rows(block, *deps):
        ahead = [from_ahead(block, "dp", step) for step in range(1, dp_count)]
        if deps:
            ahead = after(ahead, *deps)
        pieces = [block] + ahead
        return jnp.concatenate(pieces + [swapped(piece) for piece in pieces], axis=0)

    def from_mlp_rows(own_part, other_part, *deps):
        met = own_part + swapped(other_part.astype(BF)).astype(F32)
        arrivals = []
        for step in range(1, dp_count):
            block = met[step * quarter : (step + 1) * quarter].astype(BF)
            arrivals.append(to_ahead(block, "dp", step))
        if deps:
            arrivals = after(arrivals, *deps)
        total = met[:quarter]
        for block in arrivals:
            total = total + block.astype(F32)
        return total

    half_rows = dp_count * quarter
    gate_up_0 = re_laid(gate_up_halves[0])
    down_0 = re_laid(down_halves[0])
    attn_w = [attn_weights(0)]
    gate_up_w, down_w = [spread(arrived(gate_up_0))], [spread(arrived(down_0))]

    block_input, segments = after((block_input, segments), gate_up_halves[0])
    segment_rows = own_blocks(segments[:, 0, :])
    live_counts = own_blocks(live_rows[:, 0])
    allowed, cosine_table, sine_table = jax.vmap(layout)(segment_rows, live_counts)
    tables = (
        cosine_table.reshape(row_total, HEAD_SIZE),
        sine_table.reshape(row_total, HEAD_SIZE),
        allowed.astype(F32).reshape(row_total, row_count),
    )
    kernel_sizes = (dp_count, query_heads, key_heads, own_count)
    attn_flops = 2 * row_total * width * attn_columns

    current = own_blocks(block_input).reshape(row_total, width)
    current_quarter = own_quarter(current).astype(F32)
    live = (jnp.arange(row_count)[None, :] < live_counts[:, None]).reshape(row_total, 1)
    last_grad = own_blocks(cotangent).reshape(row_total, width)
    last_grad = own_quarter(jnp.where(live, last_grad, jnp.zeros_like(last_grad)))

    outputs, kept_attn, kept_mlp = [], [], []
    for section in range(sections):
        gain_attn, gain_mlp, gain_query, gain_key = gains[section]
        weight = attn_w[section]
        following = section + 1 < sections
        if following:
            next_gate_up = re_laid(gate_up_halves[section + 1])
        normed, raw, heads, mixed, attn_part = kernel_call(
            functools.partial(attn_forward_kernel, *kernel_sizes),
            place,
            weight,
            (current, gain_attn[None], gain_query[None], gain_key[None], *tables),
            [
                vmem((row_total, width), BF),
                vmem((row_total, raw_width), F32),
                vmem((row_total, raw_width), BF),
                vmem((row_total, query_width), BF),
                vmem((row_total, width), BF),
            ],
            [],
            attn_flops,
        )
        if not following:
            grad_rows = to_mlp_rows(last_grad, attn_part)
        middle = current_quarter + rows_scattered(attn_part, "tensor")
        mlp_input = root_scale(middle, gain_mlp).astype(BF)
        rows = to_mlp_rows(mlp_input)
        if following:
            gate_up_w.append(spread(arrived(next_gate_up, mlp_input)))
            next_down = re_laid(down_halves[section + 1])
        projected = dot(rows, gate_up_w[section], 1, 1)
        hidden_count = projected.shape[1] // 2
        gate_proj, up_proj = projected[:, :hidden_count], projected[:, hidden_count:]
        hidden = gated_units(gate_proj, up_proj).astype(BF)
        other_part = dot(hidden[half_rows:], down_w[section], 1, 0)
        own_part = dot(hidden[:half_rows], down_w[section], 1, 0)
        if following:
            down_w.append(spread(arrived(next_down, own_part, other_part)))
            attn_w.append(attn_weights(section + 1))
        kept_attn.append((normed, raw, heads, mixed, current_quarter, current))
        kept_mlp.append((middle, rows, gate_proj, up_proj, hidden))
        if not following:
            break
        result = (middle + from_mlp_rows(own_part, other_part)).astype(BF)
        current = rows_gathered(result, "tensor")
        current_quarter = result.astype(F32)
        outputs.append(current)

    def reduced(matrix_grad):
        shaped = matrix_grad.reshape(-1, tensor_count * part_size, width)
        met = lax.psum_scatter(shaped, "tensor", scatter_dimension=1, tiled=True)
        return by_width(met)

    def by_width(met):
        return jnp.stack(
            [met[:, :, k * block_width : (k + 1) * block_width] for k in range(dp_count)]
        )

    final_part = (own_part, other_part, middle)
    out_grad = last_grad
    grads_out, gain_sums, attn_totals, mlp_totals = [], [], [], []
    for section in reversed(range(sections)):
        gain_attn, gain_mlp, gain_query, gain_key = gains[section]
        gate_up, down = gate_up_w[section], down_w[section]
        weight = attn_w[section]
        middle, rows, gate_proj, up_proj, hidden = kept_mlp[section]
        normed, raw, heads, mixed, inside, inside_rows = kept_attn[section]
        grad_hidden = dot(grad_rows, down, 1, 1)
        _, gate_back = jax.vjp(gated_units, gate_proj, up_proj)
        grad_gate, grad_up = gate_back(grad_hidden)
        grad_gate_up = jnp.concatenate([grad_gate.astype(BF), grad_up.astype(BF)], axis=1)
        other_part = dot(grad_gate_up[half_rows:], gate_up, 1, 0)
        own_part = dot(grad_gate_up[:half_rows], gate_up, 1, 0)
        mlp_grad = from_mlp_rows(own_part, other_part)
        hidden, grad_rows, grad_gate_up, rows = after(
            (hidden, grad_rows, grad_gate_up, rows), own_part, other_part
        )
        gate_up_dot = dot(grad_gate_up, rows, 0, 0).astype(BF)
        hidden, grad_rows = after((hidden, grad_rows), gate_up_dot)
        down_dot = dot(hidden, grad_rows, 0, 0).astype(BF)
        gate_up_reduced = reduced(gate_up_dot)
        down_reduced = reduced(down_dot)
        down_total = exchanged(down_reduced, "dp")
        mlp_grad = after(mlp_grad, down_dot, gate_up_dot)

        gain_mlp_sum = jnp.sum(mlp_grad * unit_rows(middle), axis=0)
        _, middle_back = jax.vjp(lambda u: root_scale(u, gain_mlp), middle)
        middle_grad = out_grad.astype(F32) + middle_back(mlp_grad)[0]
        middle_half = middle_grad.astype(BF)
        middle_half = rows_gathered(middle_half, "tensor")
        if section + 1 == sections:
            final_own, final_other, final_middle = final_part
            result = from_mlp_rows(final_own, final_other, middle_half)
            result = (final_middle + result).astype(BF)
            outputs.append(rows_gathered(result, "tensor"))
        halves, normed_part, head_gains = kernel_call(
            functools.partial(attn_backward_kernel, *kernel_sizes),
            place,
            weight,
            (middle_half, raw, heads, gain_query[None], gain_key[None], *tables),
            [
                vmem((row_total, raw_width), BF),
                vmem((row_total, width), BF),
                vmem((2, HEAD_SIZE), F32),
            ],
            [
                pltpu.VMEM((row_total, query_width), BF),
                pltpu.VMEM((row_total, query_width + key_width), F32),
            ],
            2 * attn_flops,
        )
        gain_query_sum, gain_key_sum = head_gains[0], head_gains[1]
        normed_grad = rows_scattered(normed_part, "tensor")
        own_grad, other_grad = kernel_call(
            functools.partial(weight_grad_kernel, dp_count),
            place,
            (),
            (normed, halves, middle_half, mixed),
            [vmem((dp_count, block_width, attn_columns // 2), BF)] * 2,
            [pltpu.VMEM((block_width, attn_columns), F32)],
            attn_flops,
        )
        attn_chip = own_grad.astype(F32) + swapped(other_grad).astype(F32)
        attn_chip = attn_chip.astype(BF)
        gain_attn_sum = jnp.sum(
            normed_part.astype(F32) * unit_rows(inside_rows.astype(F32)), axis=0
        )
        _, inside_back = jax.vjp(lambda u: root_scale(u, gain_attn), inside)
        out_grad = (middle_grad + inside_back(normed_grad)[0]).astype(BF)
        grads_out.append(rows_gathered(out_grad, "tensor"))
        gain_sums.append(
            jnp.concatenate([gain_attn_sum, gain_mlp_sum, gain_query_sum, gain_key_sum])
        )
        if section:
            grad_rows = after(to_mlp_rows(out_grad), own_grad)
            gate_up_total = exchanged(gate_up_reduced, "dp")
        else:
            gate_up_total = exchanged(gate_up_reduced, "dp")
        attn_total = attn_chip[0].astype(F32)
        for step in range(1, dp_count):
            sent = to_ahead(attn_chip[step], "dp", step)
            attn_total = attn_total + sent.astype(F32)
        attn_totals.append(attn_total)
        gate_up_total, down_total = jnp.stack(gate_up_total), jnp.stack(down_total)
        mlp_totals.append([gate_up_total, down_total])
        if section:
            waiting = [gate_up_total, down_total]
        else:
            mlp_totals[0] = list(waiting)
    for held in (grads_out, gain_sums, attn_totals, mlp_totals):
        held.reverse()

    def to_owner(pair):
        keep = jnp.where(first_core, pair[0], pair[1])
        got = swapped(jnp.where(first_core, pair[1], pair[0]))
        return jnp.where(first_core, keep, got), jnp.where(first_core, got, keep)

    def gathered_output(parts):
        both = jnp.concatenate(to_owner(parts), axis=0)
        return both.reshape(1, micro_count, row_count, width)

    section_outputs = gathered_output(outputs)
    section_grads = gathered_output(grads_out)
    gain_total = jnp.stack(gain_sums)
    for axis in ("dp", "tensor", "section"):
        gain_total = summed_over(gain_total, axis)
    gain_total = jnp.where(first_core, gain_total[0], gain_total[1])[None]

    attn_both = jnp.concatenate(to_owner([t.astype(BF) for t in attn_totals]), axis=1)
    attn_both = attn_both.astype(F32)
    query_grad = attn_both[:, :query_width]
    key_grad = attn_both[:, query_width : query_width + key_width]
    value_grad = attn_both[:, query_width + key_width : raw_width]
    out_grad_w = attn_both[:, raw_width:].T

    def mlp_output(which):
        both = jnp.stack(to_owner([totals[which] for totals in mlp_totals]))
        both = jnp.moveaxis(both, 2, 0)
        return both.reshape(both.shape[0], hidden_local, block_width)

    gate_up_grad = mlp_output(0)
    down_grad = mlp_output(1)
    return (
        section_outputs,
        section_grads,
        gain_total[:, :width],
        query_grad[None],
        key_grad[None],
        value_grad[None],
        gain_total[:, 2 * width : 2 * width + HEAD_SIZE],
        gain_total[:, 2 * width + HEAD_SIZE :],
        out_grad_w[None],
        gain_total[:, width : 2 * width],
        gate_up_grad[0].T.astype(F32)[None],
        gate_up_grad[1].T.astype(F32)[None],
        down_grad[0].astype(F32)[None],
    )


def solution(mesh):
    in_specs = (
        P(None, "dp", None),
        P(None, "dp", None),
        P(None, "dp", None),
        P(None, "dp"),
        P("section", None),
        P("section", "dp", "tensor"),
        P("section", "dp", "tensor"),
        P("section", "dp", "tensor"),
        P("section", None),
        P("section", None),
        P("section", "tensor", "dp"),
        P("section", None),
        P("section", "dp", "tensor"),
        P("section", "dp", "tensor"),
        P("section", "tensor", "dp"),
    )
    out_specs = (
        P("section", None, "dp", None),
        P("section", None, "dp", None),
        P("section", None),
        P("section", "dp", "tensor"),
        P("section", "dp", "tensor"),
        P("section", "dp", "tensor"),
        P("section", None),
        P("section", None),
        P("section", "tensor", "dp"),
        P("section", None),
        P("section", "dp", "tensor"),
        P("section", "dp", "tensor"),
        P("section", "tensor", "dp"),
    )

    return jax.shard_map(
        per_device, mesh=mesh, in_specs=in_specs, out_specs=out_specs, check_vma=False
    )
```
